32 devices in a mesh: grp: 2 (over y), seq: 4 (over z), req: 2 (over x), hd: 2 (over core).
Axes of the slice: x: 2, y: 2, z: 4, core: 2. Of those that a mesh axis runs over, the one named last changes fastest.
Arguments:
- cache: bfloat16 [8, 8, 1536, 256], P(('grp', 'req'), 'hd', 'seq'), parts along dimension 0, may hold values from -7 to 7
- evicted: bfloat16 [8, 8, 256, 256], P(('grp', 'req'), 'hd', 'seq'), parts along dimension 0, may hold values from -6 to 6
- merge_weight: bfloat16 [8, 8, 256], P(('grp', 'req'), 'hd', 'seq'), parts along dimension 0, may hold values from 0.25 to 2.5
- targets: int32 [8, 8, 256], P(('grp', 'req'), 'hd', 'seq'), parts along dimension 0, may hold values from 0 to 1535, as said below
- kept_counts: int32 [8, 4], P(('grp', 'req'), 'seq'), parts along dimension 0, may hold values from 192 to 384, as said below
- queries: bfloat16 [4, 8, 64, 128], P(None, ('grp', 'req'), 'hd'), parts along dimension 1, may hold values from -1024 to 1024
- new_rows: bfloat16 [4, 8, 8, 256], P(None, ('grp', 'req'), 'hd'), parts along dimension 1, may hold values from -8 to 8
Outputs:
- merged_cache: bfloat16 [8, 8, 1536, 256], P(('grp', 'req'), 'hd', 'seq'), parts along dimension 0
- attended: bfloat16 [4, 8, 64, 128], P(None, ('grp', 'req'), 'hd'), parts along dimension 1
The draws below stay inside these ranges and needn't reach their ends.
There are 2 independent parts, one for each index of `grp`. The reference program is written for one: setup_inputs(seed, part) draws one part's arguments, and reference() takes and returns one part's arrays. A program takes and returns all parts, laid end to end along the dimension named above; each array names one. Nothing has to cross between parts.
Inputs may be any that keep to these rules, and one draw needn't show every extreme that they name: `targets`: for each request, head and block of 64 evicted rows, at most 32 rows target one block of 384 kept positions; every target is a live position. `kept_counts`: each request has a block with all 384 positions live.
All inputs are finite; a program needn't handle non-finite values.
Results may differ from the reference program's by a relative error of at most 0.0029.
Values may be sent and summed in bfloat16 or wider, within the bound.
A program may use at most 64 MiB of HBM per device.

```python
import math
import jax
import jax.numpy as jnp
from jax import lax

KVH = 8
QH = 64
HEAD = 128
KEPT_DEV = 384
EVICT_DEV = 64
STEPS = 4
REQS = 4
KEPT = 1536
EVICT = 256


def routing_tables(key):
    shards = KEPT // KEPT_DEV
    counts = jax.random.randint(jax.random.fold_in(key, 11), (REQS, shards), KEPT_DEV // 2, KEPT_DEV + 1)
    full_at = jax.random.randint(jax.random.fold_in(key, 12), (REQS,), 0, shards)
    counts = jnp.where(jnp.arange(shards)[None, :] == full_at[:, None], KEPT_DEV, counts)
    capacity = max(2, 2 * EVICT_DEV // shards)
    hottest = jax.random.randint(jax.random.fold_in(key, 13), (REQS, KVH), 0, shards)
    others_total = (shards - 1) * capacity
    spare = EVICT_DEV - capacity
    noise = jax.random.randint(jax.random.fold_in(key, 14), (REQS, KVH, shards, others_total), 0, 1 << 16)
    noise = noise * 4096 + jnp.arange(others_total)
    chosen = jnp.argsort(noise, axis=-1, stable=True)[..., :spare]
    other_dest = chosen // capacity
    other_dest = other_dest + (other_dest >= hottest[:, :, None, None]).astype(jnp.int32)
    hot_dest = jnp.broadcast_to(hottest[:, :, None, None], (REQS, KVH, shards, capacity))
    destination = jnp.concatenate([hot_dest, other_dest], axis=-1)
    shuffle = jax.random.randint(jax.random.fold_in(key, 15), (REQS, KVH, shards, EVICT_DEV), 0, 1 << 16)
    shuffle = shuffle * 4096 + jnp.arange(EVICT_DEV)
    ordering = jnp.argsort(shuffle, axis=-1, stable=True)
    destination = jnp.take_along_axis(destination, ordering, axis=-1)
    count_table = jnp.broadcast_to(counts[:, None, None, :], (REQS, KVH, shards, shards))
    limit = jnp.take_along_axis(count_table, destination, axis=-1)
    position = jax.random.randint(jax.random.fold_in(key, 16), destination.shape, 0, limit)
    aimed = destination * KEPT_DEV + position
    return (counts.astype(jnp.int32), aimed.reshape(REQS, KVH, shards * EVICT_DEV).astype(jnp.int32))


def draw_targets(key, part):
    return routing_tables(key)[1]


def draw_kept_counts(key, part):
    return routing_tables(key)[0]


def draw_cache(key, part):
    shards = KEPT // KEPT_DEV
    key_part = jnp.clip(jax.random.normal(jax.random.fold_in(key, 31), (REQS, KVH, KEPT, HEAD)), -5.0, 5.0)
    offsets = jax.random.uniform(jax.random.fold_in(key, 32), (REQS, KVH, shards, 1, HEAD), minval=-1.5, maxval=1.5)
    value_base = jnp.clip(jax.random.normal(jax.random.fold_in(key, 33), (REQS, KVH, shards, KEPT_DEV, HEAD)), -4.0, 4.0)
    value_part = (value_base + offsets).reshape(REQS, KVH, KEPT, HEAD)
    return jnp.concatenate([key_part, value_part], axis=-1).astype(jnp.bfloat16)


def decode_inputs(key):
    query_key = jax.random.fold_in(key, 21)
    fresh_key = jax.random.fold_in(key, 22)
    asked = jnp.clip(jax.random.normal(query_key, (STEPS, REQS, QH, HEAD)), -6.0, 6.0)
    fresh = jnp.clip(jax.random.normal(fresh_key, (STEPS, REQS, KVH, 2 * HEAD)), -6.0, 6.0)
    return (asked, fresh)


def draw_queries(key, part):
    return decode_inputs(key)[0].astype(jnp.bfloat16)


def draw_new_rows(key, part):
    return decode_inputs(key)[1].astype(jnp.bfloat16)


def shard_levels(rng, extent, pieces, smallest, largest):
    def one(dim, parts):
        heights = jax.random.uniform(jax.random.fold_in(jax.random.fold_in(rng, 6), dim), (parts,), jnp.float32, smallest / len(pieces), largest / len(pieces))
        return jnp.repeat(jnp.exp(heights), extent[dim] // parts).reshape((-1,) + (1,) * (len(extent) - dim - 1))

    gain = one(*pieces[0])
    for cut in pieces[1:]:
        gain = gain * one(*cut)
    return gain


def centred(rng, dims, spread, bound, pieces=(), kind=jnp.bfloat16):
    array = jax.random.normal(rng, dims, jnp.float32) * spread
    if len(pieces) > 0:
        array = shard_levels(rng, dims, pieces, -0.22, 0.18) * array
    return jnp.clip(array, min=-bound, max=bound).astype(kind)


def setup_inputs(seed: int = 0, part: int = 0) -> dict:
    splits = jax.random.split(jax.random.key(seed), 8)
    own_keys = jax.random.split(jax.random.fold_in(splits[7], part), 8)
    return {
        "cache": draw_cache(jax.random.fold_in(jax.random.fold_in(splits[7], part), 71), part),
        "evicted": centred(own_keys[1], (REQS, KVH, EVICT, 2 * HEAD), 1.0, 6.0, ((0, 2), (1, 2), (2, 4))),
        "merge_weight": jnp.clip(jnp.exp(math.log(2.5) - 2.3025851 * jax.random.uniform(own_keys[2], (REQS, KVH, EVICT), jnp.float32) ** shard_levels(own_keys[2], (REQS, KVH, EVICT), ((0, 2), (1, 2), (2, 4)), -0.2, 0.2)), 0.25, 2.5).astype(jnp.bfloat16),
        "targets": draw_targets(jax.random.fold_in(jax.random.fold_in(splits[7], part), 71), part),
        "kept_counts": draw_kept_counts(jax.random.fold_in(jax.random.fold_in(splits[7], part), 71), part),
        "queries": draw_queries(jax.random.fold_in(jax.random.fold_in(splits[7], part), 71), part),
        "new_rows": draw_new_rows(jax.random.fold_in(jax.random.fold_in(splits[7], part), 71), part),
    }


def merge_head(inputs):
    stored, removed, weights, target_rows = inputs
    weight_f = weights.astype(jnp.float32)
    summed = jax.ops.segment_sum(weight_f[:, None] * removed.astype(jnp.float32), target_rows, num_segments=KEPT)
    weight_sum = jax.ops.segment_sum(weight_f, target_rows, num_segments=KEPT)
    return ((stored.astype(jnp.float32) + summed) / (1.0 + weight_sum)[:, None]).astype(jnp.bfloat16)

def round_weights(values):
    rounded = values.astype(jnp.bfloat16)
    rounded = lax.optimization_barrier(rounded)
    return rounded.astype(jnp.float32)

def attend_request(inputs):
    stored, counts, asked_rows, fresh_rows = inputs
    group_size = QH // KVH
    blocks_count = KEPT // KEPT_DEV
    scale_factor = 1.0 / math.sqrt(HEAD)
    query_rows = asked_rows.reshape(STEPS, KVH, group_size, HEAD).transpose(1, 0, 2, 3)
    query_rows = query_rows.reshape(KVH, STEPS * group_size, HEAD).astype(jnp.float32)
    key_blocks = stored[:, :, :HEAD].astype(jnp.float32).reshape(KVH, blocks_count, KEPT_DEV, HEAD)
    value_blocks = stored[:, :, HEAD:].astype(jnp.float32).reshape(KVH, blocks_count, KEPT_DEV, HEAD)
    scores = jnp.einsum('hqd,hbkd->hbqk', query_rows, key_blocks) * scale_factor
    living = jnp.arange(KEPT_DEV, dtype=jnp.int32)[None, :] < counts[:, None]
    scores = jnp.where(living[None, :, None, :], scores, -1e+30)
    block_max = lax.optimization_barrier(jnp.max(scores, axis=-1))
    exponent = jnp.exp(scores - block_max[..., None])
    block_sum = lax.optimization_barrier(jnp.sum(exponent, axis=-1))
    block_acc = jnp.einsum('hbqk,hbkd->hbqd', round_weights(exponent), value_blocks)
    fresh_heads = fresh_rows.transpose(1, 0, 2).astype(jnp.float32)
    new_scores = jnp.einsum('hqd,hjd->hqj', query_rows, fresh_heads[:, :, :HEAD]) * scale_factor
    step_index = jnp.arange(STEPS * group_size, dtype=jnp.int32) // group_size
    allowed = jnp.arange(STEPS, dtype=jnp.int32)[None, :] <= step_index[:, None]
    new_scores = jnp.where(allowed[None], new_scores, -1e+30)
    new_max = lax.optimization_barrier(jnp.max(new_scores, axis=-1))
    new_exponent = jnp.exp(new_scores - new_max[..., None])
    new_sum = lax.optimization_barrier(jnp.sum(new_exponent, axis=-1))
    new_acc = jnp.einsum('hqj,hjd->hqd', round_weights(new_exponent), fresh_heads[:, :, HEAD:])
    highest = jnp.maximum(lax.optimization_barrier(jnp.max(block_max, axis=1)), new_max)
    block_scale = jnp.exp(block_max - highest[:, None, :])
    new_scale = jnp.exp(new_max - highest)
    denominator = lax.optimization_barrier(jnp.sum(block_sum * block_scale, axis=1)) + new_sum * new_scale
    numerator = lax.optimization_barrier(jnp.sum(block_acc * block_scale[..., None], axis=1)) + new_acc * new_scale[..., None]
    result = (numerator / denominator[..., None]).astype(jnp.bfloat16)
    result = result.reshape(KVH, STEPS, group_size, HEAD).transpose(1, 0, 2, 3)
    return result.reshape(STEPS, QH, HEAD)

def reference(cache, evicted, merge_weight, targets, kept_counts, queries, new_rows):
    merged_flat = lax.map(merge_head, (cache.reshape(REQS * KVH, KEPT, 2 * HEAD), evicted.reshape(REQS * KVH, EVICT, 2 * HEAD), merge_weight.reshape(REQS * KVH, EVICT), targets.reshape(REQS * KVH, EVICT)))
    merged_cache = merged_flat.reshape(REQS, KVH, KEPT, 2 * HEAD)
    attended = lax.map(attend_request, (merged_cache, kept_counts, queries.transpose(1, 0, 2, 3), new_rows.transpose(1, 0, 2, 3)))
    return (merged_cache, attended.transpose(1, 0, 2, 3))
```

```python
import functools
import math

import jax
import jax.numpy as jnp
from jax import lax
from jax.experimental import pallas as pl
from jax.experimental.pallas import tpu as pltpu
from jax.sharding import PartitionSpec as P

F32 = jnp.float32
BF16 = jnp.bfloat16
NEG = -1e30


def contract_last(a, b):
    return lax.dot_general(a, b, (((1,), (1,)), ((), ())), preferred_element_type=F32)


def softmax_block(query, keys, values, allowed, scale):
    scores = jnp.where(allowed, contract_last(query, keys) * scale, NEG)
    highest = jnp.max(scores, axis=-1, keepdims=True)
    exponent = jnp.exp(scores - highest)
    total = jnp.sum(exponent, axis=-1, keepdims=True)
    weighted = jnp.dot(exponent.astype(BF16), values, preferred_element_type=F32)
    return highest, total, weighted


def kernel(
    shards, cap, groups, owners,
    cache, evicted, weight, target, counts, queries, fresh,
    merged, attended,
    cache_v, evict_v, weight_v, target_v, counts_v, query_v, fresh_v,
    send, recv, meta_send, meta_recv, query_s, fresh_o, fresh_ml,
    part, part_recv, result, attended_v,
    in_sem, cache_sem, out_sem, att_sem, row_ssem, row_rsem, meta_ssem, meta_rsem,
    part_ssem, part_rsem, res_ssem, res_rsem,
):
    reqs, heads, kept, width = cache_v.shape
    pairs = reqs * heads
    evict = evict_v.shape[2]
    steps, _, _, depth = query_v.shape
    rows = query_s.shape[1]
    group = rows // steps
    slots = shards * cap
    per = pairs // owners
    scale = 1.0 / math.sqrt(depth)
    me = lax.axis_index("seq")

    def peer(d):
        return lax.rem(me + d, shards)

    def source(d):
        return lax.rem(me + shards - d, shards)

    def remote(src, dst, ssem, rsem, device):
        return pltpu.make_async_remote_copy(
            src_ref=src, dst_ref=dst, send_sem=ssem, recv_sem=rsem,
            device_id={"seq": device}, device_id_type=pl.DeviceIdType.MESH,
        )

    small = [
        pltpu.make_async_copy(src, dst, in_sem.at[i])
        for i, (src, dst) in enumerate((
            (target, target_v), (weight, weight_v), (evicted, evict_v),
            (queries, query_v), (fresh, fresh_v), (counts, counts_v),
        ))
    ]
    for copy in small:
        copy.start()
    order = []
    for o in [0] + list(range(owners - 1, 0, -1)):
        order += [o * per + j for j in range(per)]
    loads = {}
    for i in order:
        r, h = divmod(i, heads)
        loads[i] = pltpu.make_async_copy(cache.at[r, h], cache_v.at[r, h], cache_sem.at[i])
        loads[i].start()

    barrier = pltpu.get_barrier_semaphore()
    for d in range(1, shards):
        pl.semaphore_signal(
            barrier, inc=1, device_id={"seq": peer(d)}, device_id_type=pl.DeviceIdType.MESH
        )

    for copy in small[:3]:
        copy.wait()
    aimed = jnp.concatenate([target_v[r] for r in range(reqs)], axis=0)
    weights = jnp.concatenate([weight_v[r].astype(F32) for r in range(reqs)], axis=0)
    owned, position, base = [], jnp.zeros_like(aimed), jnp.zeros(aimed.shape, F32)
    for d in range(shards):
        low = peer(d) * kept
        mine = (aimed >= low) & (aimed < low + kept)
        owned.append(jnp.where(mine, 1.0, 0.0))
        position = jnp.where(mine, aimed - low, position)
        base = jnp.where(mine, float(d * cap), base)
    above = lax.broadcasted_iota(jnp.int32, (evict, evict), 0) < lax.broadcasted_iota(
        jnp.int32, (evict, evict), 1
    )
    earlier = jnp.dot(
        jnp.concatenate(owned, axis=0).astype(BF16),
        jnp.where(above, 1.0, 0.0).astype(BF16),
        preferred_element_type=F32,
    )
    slot = base
    for d in range(shards):
        slot = slot + owned[d] * earlier[d * pairs : (d + 1) * pairs]
    slot = slot.astype(jnp.int32)
    features = jnp.concatenate(
        [weights, (position & 255).astype(F32), (position >> 8).astype(F32)], axis=0
    ).astype(BF16)
    slot_row = lax.broadcasted_iota(jnp.int32, (slots, evict), 0)
    for i in order:
        r, h = divmod(i, heads)
        packing = jnp.where(slot_row == slot[i : i + 1, :], 1.0, 0.0).astype(BF16)
        packed = jnp.dot(packing, evict_v[r, h], preferred_element_type=F32).astype(BF16)
        send[i] = packed
        recv[i, 0:cap, :] = packed[0:cap]
        meta = contract_last(features, packing)
        meta_send[i : i + 1, :] = meta[i : i + 1]
        meta_send[pairs + i : pairs + i + 1, :] = (
            meta[2 * pairs + i : 2 * pairs + i + 1] * 256.0 + meta[pairs + i : pairs + i + 1]
        )

    pl.semaphore_wait(barrier, shards - 1)

    meta_copies = {}
    for d in range(1, shards):
        meta_copies[d] = remote(
            meta_send, meta_recv.at[d], meta_ssem.at[d], meta_rsem.at[d], peer(d)
        )
        meta_copies[d].start()
    span = pairs // groups
    row_copies = {}
    for g in range(groups):
        first = order[g] if groups == pairs else g * span
        for d in range(1, shards):
            lot = (pl.ds(first, span), pl.ds(d * cap, cap))
            row_copies[first, d] = remote(
                send.at[lot], recv.at[lot], row_ssem.at[g, d], row_rsem.at[g, d], peer(d)
            )
            row_copies[first, d].start()

    for copy in small[3:]:
        copy.wait()
    diagonal = lax.broadcasted_iota(jnp.int32, (rows, 128), 0) == lax.broadcasted_iota(
        jnp.int32, (rows, 128), 1
    )

    def to_rows(*columns):
        flat = [jnp.sum(jnp.where(diagonal, c, 0.0), axis=0, keepdims=True) for c in columns]
        return jnp.concatenate(flat + [jnp.zeros((8 - len(flat), 128), F32)], axis=0)

    def to_column(row):
        return jnp.sum(jnp.where(diagonal, row, 0.0), axis=1, keepdims=True)

    padded = -(-steps // 16) * 16
    new_step = lax.broadcasted_iota(jnp.int32, (rows, padded), 1)
    row_index = lax.broadcasted_iota(jnp.int32, (rows, padded), 0)
    allowed = row_index < 0
    for s in range(steps):
        allowed = allowed | ((new_step == s) & (row_index >= s * group))
    for r in range(reqs):
        asked = [query_v[s, r].astype(F32) for s in range(steps)]
        added = [fresh_v[s, r].astype(F32) for s in range(steps)]
        for h in range(heads):
            i = r * heads + h
            query = jnp.concatenate(
                [a[h * group : (h + 1) * group] for a in asked], axis=0
            ).astype(BF16)
            query_s[i] = query
            latest = jnp.concatenate(
                [a[h : h + 1] for a in added] + [jnp.zeros((padded - steps, width), F32)], axis=0
            ).astype(BF16)
            highest, total, weighted = softmax_block(
                query, latest[:, :depth], latest[:, depth:], allowed, scale
            )
            fresh_o[i] = weighted
            fresh_ml[i] = to_rows(highest, total)

    for d in range(1, shards):
        meta_copies[d].wait_recv()
    lane = lax.broadcasted_iota(jnp.int32, (2 * pairs, slots), 1)
    meta = meta_send[...]
    for d in range(1, shards):
        meta = jnp.where(lane >= d * cap, meta_recv[d], meta)
    slot_weight = meta[:pairs]
    slot_position = meta[pairs:].astype(jnp.int32)

    kept_row = lax.broadcasted_iota(jnp.int32, (kept, slots), 0)
    kept_lane = lax.broadcasted_iota(jnp.int32, (rows, kept), 1)
    ones = jnp.ones((slots, 128), BF16)
    stores = []
    for n, i in enumerate(order):
        r, h = divmod(i, heads)
        loads[i].wait()
        if groups == pairs:
            for d in range(1, shards):
                row_copies[i, d].wait_recv()
        elif n == 0:
            for copy in row_copies.values():
                copy.wait_recv()
        placing = jnp.where(
            kept_row == slot_position[i : i + 1], slot_weight[i : i + 1], 0.0
        ).astype(BF16)
        summed = jnp.dot(placing, recv[i], preferred_element_type=F32)
        factor = 1.0 / (1.0 + jnp.dot(placing, ones, preferred_element_type=F32))
        factor = jnp.concatenate([factor] * (width // 128), axis=1)
        fused = ((cache_v[r, h].astype(F32) + summed) * factor).astype(BF16)
        cache_v[r, h] = fused
        store = pltpu.make_async_copy(cache_v.at[r, h], merged.at[r, h], out_sem.at[i])
        store.start()
        stores.append(store)
        highest, total, weighted = softmax_block(
            query_s[i], fused[:, :depth], fused[:, depth:], kept_lane < counts_v[r : r + 1, :], scale
        )
        part[i, 0:rows, :] = weighted
        part[i, rows : rows + 8, :] = to_rows(highest, total)
        owner, j = divmod(i, per)
        away = lax.rem(owner - me + shards, shards)

        @pl.when(me != owner)
        def _():
            remote(
                part.at[i], part_recv.at[j, away], part_ssem.at[i], part_rsem.at[j, away], owner
            ).start()

    def part_in(j, d):
        return remote(
            part.at[j], part_recv.at[j, d], part_ssem.at[j], part_rsem.at[j, d], peer(d)
        )

    def res_out(j, d):
        mine = me * per + j
        return remote(
            result.at[mine], result.at[mine], res_ssem.at[j, d], res_rsem.at[j, d], peer(d)
        )

    def res_in(j, d):
        theirs = source(d) * per + j
        return remote(
            result.at[theirs], result.at[theirs], res_ssem.at[j, d], res_rsem.at[j, d], peer(d)
        )

    def only_owners(index, f):
        if owners == shards:
            f()
        else:
            pl.when(index < owners)(f)

    def combine():
        for j in range(per):
            mine = me * per + j
            for d in range(1, shards):
                part_in(j, d).wait_recv()
            tiles = [fresh_ml[mine], part[mine, rows : rows + 8, :]]
            outs = [fresh_o[mine], part[mine, 0:rows, :]]
            for d in range(1, shards):
                tiles.append(part_recv[j, d, rows : rows + 8, :])
                outs.append(part_recv[j, d, 0:rows, :])
            top = tiles[0][0:1]
            for tile in tiles[1:]:
                top = jnp.maximum(top, tile[0:1])
            shares = [jnp.exp(tile[0:1] - top) for tile in tiles]
            total = shares[0] * tiles[0][1:2]
            for share, tile in zip(shares[1:], tiles[1:]):
                total = total + share * tile[1:2]
            lanes = lax.broadcasted_iota(jnp.int32, total.shape, 1)
            total = jnp.where(lanes < rows, total, 1.0)
            blend = to_column(shares[0] / total) * outs[0]
            for share, out in zip(shares[1:], outs[1:]):
                blend = blend + to_column(share / total) * out
            result[mine] = blend.astype(BF16)
            for d in range(1, shards):
                res_out(j, d).start()

    only_owners(me, combine)

    for j in range(per):
        for d in range(1, shards):
            only_owners(source(d), lambda: res_in(j, d).wait_recv())
    for r in range(reqs):
        done = [result[r * heads + h].astype(F32) for h in range(heads)]
        for s in range(steps):
            attended_v[s, r] = jnp.concatenate(
                [a[s * group : (s + 1) * group] for a in done], axis=0
            ).astype(BF16)
    last = pltpu.make_async_copy(attended_v, attended, att_sem.at[0])
    last.start()

    for copy in list(meta_copies.values()) + list(row_copies.values()):
        copy.wait_send()
    for i in order:
        owner = i // per

        @pl.when(me != owner)
        def _():
            remote(
                part.at[i], part_recv.at[0, 1], part_ssem.at[i], part_rsem.at[0, 1], owner
            ).wait_send()

    def drain():
        for j in range(per):
            for d in range(1, shards):
                res_out(j, d).wait_send()

    only_owners(me, drain)
    for store in stores:
        store.wait()
    last.wait()


def body(shards, cache, evicted, merge_weight, targets, kept_counts, queries, new_rows):
    reqs, heads, kept, width = cache.shape
    pairs = reqs * heads
    evict = evicted.shape[2]
    steps, _, query_local, depth = queries.shape
    rows = steps * query_local // heads
    cap = -(-max(2, 2 * evict // shards) // 16) * 16
    slots = shards * cap
    groups = pairs if shards <= 8 else 1
    owners = min(shards, pairs)
    per = pairs // owners
    dma = pltpu.SemaphoreType.DMA
    return pl.pallas_call(
        functools.partial(kernel, shards, cap, groups, owners),
        out_shape=(
            jax.ShapeDtypeStruct(cache.shape, BF16),
            jax.ShapeDtypeStruct(queries.shape, BF16),
        ),
        in_specs=[pl.BlockSpec(memory_space=pl.ANY)] * 7,
        out_specs=(pl.BlockSpec(memory_space=pl.ANY),) * 2,
        scratch_shapes=[
            pltpu.VMEM(cache.shape, BF16),
            pltpu.VMEM(evicted.shape, BF16),
            pltpu.VMEM(merge_weight.shape, BF16),
            pltpu.VMEM(targets.shape, jnp.int32),
            pltpu.VMEM(kept_counts.shape, jnp.int32),
            pltpu.VMEM(queries.shape, BF16),
            pltpu.VMEM(new_rows.shape, BF16),
            pltpu.VMEM((pairs, slots, width), BF16),
            pltpu.VMEM((pairs, slots, width), BF16),
            pltpu.VMEM((2 * pairs, slots), F32),
            pltpu.VMEM((shards, 2 * pairs, slots), F32),
            pltpu.VMEM((pairs, rows, depth), BF16),
            pltpu.VMEM((pairs, rows, depth), F32),
            pltpu.VMEM((pairs, 8, 128), F32),
            pltpu.VMEM((pairs, rows + 8, depth), F32),
            pltpu.VMEM((per, shards, rows + 8, depth), F32),
            pltpu.VMEM((pairs, rows, depth), BF16),
            pltpu.VMEM(queries.shape, BF16),
            dma((6,)),
            dma((pairs,)),
            dma((pairs,)),
            dma((1,)),
            dma((groups, shards)),
            dma((groups, shards)),
            dma((shards,)),
            dma((shards,)),
            dma((pairs,)),
            dma((per, shards)),
            dma((per, shards)),
            dma((per, shards)),
        ],
        compiler_params=pltpu.CompilerParams(
            collective_id=0, has_side_effects=True, vmem_limit_bytes=48 * 1024 * 1024
        ),
    )(cache, evicted, merge_weight, targets, kept_counts, queries, new_rows)


def solution(mesh):
    return jax.shard_map(
        functools.partial(body, mesh.shape["seq"]),
        mesh=mesh,
        in_specs=(
            P(("grp", "req"), "hd", "seq", None),
            P(("grp", "req"), "hd", "seq", None),
            P(("grp", "req"), "hd", "seq"),
            P(("grp", "req"), "hd", "seq"),
            P(("grp", "req"), "seq"),
            P(None, ("grp", "req"), "hd", None),
            P(None, ("grp", "req"), "hd", None),
        ),
        out_specs=(P(("grp", "req"), "hd", "seq", None), P(None, ("grp", "req"), "hd", None)),
        check_vma=False,
    )
```

```python
import functools
import math

import jax
import jax.numpy as jnp
from jax import lax
from jax.experimental import pallas as pl
from jax.experimental.pallas import tpu as pltpu
from jax.sharding import PartitionSpec as P

F32 = jnp.float32
BF16 = jnp.bfloat16
NEG = -1e30


def contract_last(a, b):
    return lax.dot_general(a, b, (((1,), (1,)), ((), ())), preferred_element_type=F32)


def softmax_block(query, keys, values, allowed, scale):
    scores = jnp.where(allowed, contract_last(query, keys) * scale, NEG)
    highest = jnp.max(scores, axis=-1, keepdims=True)
    exponent = jnp.exp(scores - highest)
    total = jnp.sum(exponent, axis=-1, keepdims=True)
    weighted = jnp.dot(exponent.astype(BF16), values, preferred_element_type=F32)
    return highest, total, weighted


def kernel(
    shards, cap, groups, owners,
    cache, evicted, weight, target, counts, queries, fresh,
    merged, attended,
    evict_v, weight_v, target_v, counts_v, query_v, fresh_v,
    send, recv, meta_send, meta_recv, query_s, fresh_o, fresh_ml,
    part, part_recv, result,
    in_sem, cache_sem, row_ssem, row_rsem, meta_ssem, meta_rsem,
    part_ssem, part_rsem, res_ssem, res_rsem,
):
    reqs, heads, kept, width = merged.shape
    pairs = reqs * heads
    evict = evict_v.shape[2]
    steps, _, _, depth = query_v.shape
    rows = query_s.shape[1]
    group = rows // steps
    slots = shards * cap
    per = pairs // owners
    scale = 1.0 / math.sqrt(depth)
    me = lax.axis_index("seq")

    def peer(d):
        return lax.rem(me + d, shards)

    def source(d):
        return lax.rem(me + shards - d, shards)

    def remote(src, dst, ssem, rsem, device):
        return pltpu.make_async_remote_copy(
            src_ref=src, dst_ref=dst, send_sem=ssem, recv_sem=rsem,
            device_id={"seq": device}, device_id_type=pl.DeviceIdType.MESH,
        )

    small = [
        pltpu.make_async_copy(src, dst, in_sem.at[i])
        for i, (src, dst) in enumerate((
            (target, target_v), (weight, weight_v), (evicted, evict_v),
            (queries, query_v), (fresh, fresh_v), (counts, counts_v),
        ))
    ]
    for copy in small:
        copy.start()
    order = []
    for o in [0] + list(range(owners - 1, 0, -1)):
        order += [o * per + j for j in range(per)]
    loads = {}
    for i in order:
        r, h = divmod(i, heads)
        loads[i] = pltpu.make_async_copy(cache.at[r, h], merged.at[r, h], cache_sem.at[i])
        loads[i].start()

    barrier = pltpu.get_barrier_semaphore()
    for d in range(1, shards):
        pl.semaphore_signal(
            barrier, inc=1, device_id={"seq": peer(d)}, device_id_type=pl.DeviceIdType.MESH
        )

    for copy in small[:3]:
        copy.wait()
    aimed = jnp.concatenate([target_v[r] for r in range(reqs)], axis=0)
    weights = jnp.concatenate([weight_v[r].astype(F32) for r in range(reqs)], axis=0)
    owned, position, base = [], jnp.zeros_like(aimed), jnp.zeros(aimed.shape, F32)
    for d in range(shards):
        low = peer(d) * kept
        mine = (aimed >= low) & (aimed < low + kept)
        owned.append(jnp.where(mine, 1.0, 0.0))
        position = jnp.where(mine, aimed - low, position)
        base = jnp.where(mine, float(d * cap), base)
    above = lax.broadcasted_iota(jnp.int32, (evict, evict), 0) < lax.broadcasted_iota(
        jnp.int32, (evict, evict), 1
    )
    earlier = jnp.dot(
        jnp.concatenate(owned, axis=0).astype(BF16),
        jnp.where(above, 1.0, 0.0).astype(BF16),
        preferred_element_type=F32,
    )
    slot = base
    for d in range(shards):
        slot = slot + owned[d] * earlier[d * pairs : (d + 1) * pairs]
    slot = slot.astype(jnp.int32)
    features = jnp.concatenate(
        [weights, (position & 255).astype(F32), (position >> 8).astype(F32)], axis=0
    ).astype(BF16)
    slot_row = lax.broadcasted_iota(jnp.int32, (slots, evict), 0)
    for i in order:
        r, h = divmod(i, heads)
        packing = jnp.where(slot_row == slot[i : i + 1, :], 1.0, 0.0).astype(BF16)
        packed = jnp.dot(packing, evict_v[r, h], preferred_element_type=F32).astype(BF16)
        send[i] = packed
        recv[i, 0:cap, :] = packed[0:cap]
        meta = contract_last(features, packing)
        meta_send[i : i + 1, :] = meta[i : i + 1]
        meta_send[pairs + i : pairs + i + 1, :] = (
            meta[2 * pairs + i : 2 * pairs + i + 1] * 256.0 + meta[pairs + i : pairs + i + 1]
        )

    pl.semaphore_wait(barrier, shards - 1)

    meta_copies = {}
    for d in range(1, shards):
        meta_copies[d] = remote(
            meta_send, meta_recv.at[d], meta_ssem.at[d], meta_rsem.at[d], peer(d)
        )
        meta_copies[d].start()
    span = pairs // groups
    row_copies = {}
    for g in range(groups):
        first = order[g] if groups == pairs else g * span
        for d in range(1, shards):
            lot = (pl.ds(first, span), pl.ds(d * cap, cap))
            row_copies[first, d] = remote(
                send.at[lot], recv.at[lot], row_ssem.at[g, d], row_rsem.at[g, d], peer(d)
            )
            row_copies[first, d].start()

    for copy in small[3:]:
        copy.wait()
    diagonal = lax.broadcasted_iota(jnp.int32, (rows, 128), 0) == lax.broadcasted_iota(
        jnp.int32, (rows, 128), 1
    )

    def to_rows(*columns):
        flat = [jnp.sum(jnp.where(diagonal, c, 0.0), axis=0, keepdims=True) for c in columns]
        return jnp.concatenate(flat + [jnp.zeros((8 - len(flat), 128), F32)], axis=0)

    def to_column(row):
        return jnp.sum(jnp.where(diagonal, row, 0.0), axis=1, keepdims=True)

    padded = -(-steps // 16) * 16
    new_step = lax.broadcasted_iota(jnp.int32, (rows, padded), 1)
    row_index = lax.broadcasted_iota(jnp.int32, (rows, padded), 0)
    allowed = row_index < 0
    for s in range(steps):
        allowed = allowed | ((new_step == s) & (row_index >= s * group))
    for r in range(reqs):
        asked = [query_v[s, r].astype(F32) for s in range(steps)]
        added = [fresh_v[s, r].astype(F32) for s in range(steps)]
        for h in range(heads):
            i = r * heads + h
            query = jnp.concatenate(
                [a[h * group : (h + 1) * group] for a in asked], axis=0
            ).astype(BF16)
            query_s[i] = query
            latest = jnp.concatenate(
                [a[h : h + 1] for a in added] + [jnp.zeros((padded - steps, width), F32)], axis=0
            ).astype(BF16)
            highest, total, weighted = softmax_block(
                query, latest[:, :depth], latest[:, depth:], allowed, scale
            )
            fresh_o[i] = weighted
            fresh_ml[i] = to_rows(highest, total)

    for d in range(1, shards):
        meta_copies[d].wait_recv()
    lane = lax.broadcasted_iota(jnp.int32, (2 * pairs, slots), 1)
    meta = meta_send[...]
    for d in range(1, shards):
        meta = jnp.where(lane >= d * cap, meta_recv[d], meta)
    slot_weight = meta[:pairs]
    slot_position = meta[pairs:].astype(jnp.int32)

    kept_row = lax.broadcasted_iota(jnp.int32, (kept, slots), 0)
    kept_lane = lax.broadcasted_iota(jnp.int32, (rows, kept), 1)
    ones = jnp.ones((slots, 128), BF16)
    for n, i in enumerate(order):
        r, h = divmod(i, heads)
        loads[i].wait()
        if groups == pairs:
            for d in range(1, shards):
                row_copies[i, d].wait_recv()
        elif n == 0:
            for copy in row_copies.values():
                copy.wait_recv()
        placing = jnp.where(
            kept_row == slot_position[i : i + 1], slot_weight[i : i + 1], 0.0
        ).astype(BF16)
        summed = jnp.dot(placing, recv[i], preferred_element_type=F32)
        factor = 1.0 / (1.0 + jnp.dot(placing, ones, preferred_element_type=F32))
        factor = jnp.concatenate([factor] * (width // 128), axis=1)
        fused = ((merged[r, h].astype(F32) + summed) * factor).astype(BF16)
        merged[r, h] = fused
        highest, total, weighted = softmax_block(
            query_s[i], fused[:, :depth], fused[:, depth:], kept_lane < counts_v[:, r : r + 1], scale
        )
        part[i, 0:rows, :] = weighted
        part[i, rows : rows + 8, :] = to_rows(highest, total)
        owner, j = divmod(i, per)
        away = lax.rem(owner - me + shards, shards)

        @pl.when(me != owner)
        def _():
            remote(
                part.at[i], part_recv.at[j, away], part_ssem.at[i], part_rsem.at[j, away], owner
            ).start()

    def part_in(j, d):
        return remote(
            part.at[j], part_recv.at[j, d], part_ssem.at[j], part_rsem.at[j, d], peer(d)
        )

    def res_out(j, d):
        mine = me * per + j
        return remote(
            result.at[mine], result.at[mine], res_ssem.at[j, d], res_rsem.at[j, d], peer(d)
        )

    def res_in(j, d):
        theirs = source(d) * per + j
        return remote(
            result.at[theirs], result.at[theirs], res_ssem.at[j, d], res_rsem.at[j, d], peer(d)
        )

    def only_owners(index, f):
        if owners == shards:
            f()
        else:
            pl.when(index < owners)(f)

    def combine():
        for j in range(per):
            mine = me * per + j
            for d in range(1, shards):
                part_in(j, d).wait_recv()
            tiles = [fresh_ml[mine], part[mine, rows : rows + 8, :]]
            outs = [fresh_o[mine], part[mine, 0:rows, :]]
            for d in range(1, shards):
                tiles.append(part_recv[j, d, rows : rows + 8, :])
                outs.append(part_recv[j, d, 0:rows, :])
            top = tiles[0][0:1]
            for tile in tiles[1:]:
                top = jnp.maximum(top, tile[0:1])
            shares = [jnp.exp(tile[0:1] - top) for tile in tiles]
            total = shares[0] * tiles[0][1:2]
            for share, tile in zip(shares[1:], tiles[1:]):
                total = total + share * tile[1:2]
            lanes = lax.broadcasted_iota(jnp.int32, total.shape, 1)
            total = jnp.where(lanes < rows, total, 1.0)
            blend = to_column(shares[0] / total) * outs[0]
            for share, out in zip(shares[1:], outs[1:]):
                blend = blend + to_column(share / total) * out
            result[mine] = blend.astype(BF16)
            for d in range(1, shards):
                res_out(j, d).start()

    only_owners(me, combine)

    for j in range(per):
        for d in range(1, shards):
            only_owners(source(d), lambda: res_in(j, d).wait_recv())
    for r in range(reqs):
        done = [result[r * heads + h].astype(F32) for h in range(heads)]
        for s in range(steps):
            attended[s, r] = jnp.concatenate(
                [a[s * group : (s + 1) * group] for a in done], axis=0
            ).astype(BF16)

    for copy in list(meta_copies.values()) + list(row_copies.values()):
        copy.wait_send()
    for i in order:
        owner = i // per

        @pl.when(me != owner)
        def _():
            remote(
                part.at[i], part_recv.at[0, 1], part_ssem.at[i], part_rsem.at[0, 1], owner
            ).wait_send()

    def drain():
        for j in range(per):
            for d in range(1, shards):
                res_out(j, d).wait_send()

    only_owners(me, drain)


def write_out(merged, attended, merged_out, attended_out, sem):
    copies = [
        pltpu.make_async_copy(merged, merged_out, sem.at[0]),
        pltpu.make_async_copy(attended, attended_out, sem.at[1]),
    ]
    for copy in copies:
        copy.start()
    for copy in copies:
        copy.wait()


def body(shards, cache, evicted, merge_weight, targets, kept_counts, queries, new_rows):
    reqs, heads, kept, width = cache.shape
    pairs = reqs * heads
    evict = evicted.shape[2]
    steps, _, query_local, depth = queries.shape
    rows = steps * query_local // heads
    cap = -(-max(2, 2 * evict // shards) // 16) * 16
    slots = shards * cap
    groups = pairs if shards <= 8 else 1
    owners = min(shards, pairs)
    per = pairs // owners
    dma = pltpu.SemaphoreType.DMA
    done = pl.pallas_call(
        functools.partial(kernel, shards, cap, groups, owners),
        out_shape=(
            jax.ShapeDtypeStruct(cache.shape, BF16),
            jax.ShapeDtypeStruct(queries.shape, BF16),
        ),
        in_specs=[pl.BlockSpec(memory_space=pltpu.HBM)] * 7,
        out_specs=(pl.BlockSpec(memory_space=pltpu.VMEM),) * 2,
        scratch_shapes=[
            pltpu.VMEM(evicted.shape, BF16),
            pltpu.VMEM(merge_weight.shape, BF16),
            pltpu.VMEM(targets.shape, jnp.int32),
            pltpu.VMEM(kept_counts.shape[::-1], jnp.int32),
            pltpu.VMEM(queries.shape, BF16),
            pltpu.VMEM(new_rows.shape, BF16),
            pltpu.VMEM((pairs, slots, width), BF16),
            pltpu.VMEM((pairs, slots, width), BF16),
            pltpu.VMEM((2 * pairs, slots), F32),
            pltpu.VMEM((shards, 2 * pairs, slots), F32),
            pltpu.VMEM((pairs, rows, depth), BF16),
            pltpu.VMEM((pairs, rows, depth), F32),
            pltpu.VMEM((pairs, 8, 128), F32),
            pltpu.VMEM((pairs, rows + 8, depth), F32),
            pltpu.VMEM((per, shards, rows + 8, depth), F32),
            pltpu.VMEM((pairs, rows, depth), BF16),
            dma((6,)),
            dma((pairs,)),
            dma((groups, shards)),
            dma((groups, shards)),
            dma((shards,)),
            dma((shards,)),
            dma((pairs,)),
            dma((per, shards)),
            dma((per, shards)),
            dma((per, shards)),
        ],
        compiler_params=pltpu.CompilerParams(
            collective_id=0, has_side_effects=True, vmem_limit_bytes=48 * 1024 * 1024
        ),
    )(*(
        pltpu.with_memory_space_constraint(a, pltpu.HBM)
        for a in (cache, evicted, merge_weight, targets, kept_counts.T, queries, new_rows)
    ))
    return pl.pallas_call(
        write_out,
        out_shape=tuple(jax.ShapeDtypeStruct(a.shape, a.dtype) for a in done),
        in_specs=[pl.BlockSpec(memory_space=pltpu.VMEM)] * 2,
        out_specs=(pl.BlockSpec(memory_space=pltpu.HBM),) * 2,
        scratch_shapes=[dma((2,))],
    )(*(pltpu.with_memory_space_constraint(a, pltpu.VMEM) for a in done))


def solution(mesh):
    return jax.shard_map(
        functools.partial(body, mesh.shape["seq"]),
        mesh=mesh,
        in_specs=(
            P(("grp", "req"), "hd", "seq", None),
            P(("grp", "req"), "hd", "seq", None),
            P(("grp", "req"), "hd", "seq"),
            P(("grp", "req"), "hd", "seq"),
            P(("grp", "req"), "seq"),
            P(None, ("grp", "req"), "hd", None),
            P(None, ("grp", "req"), "hd", None),
        ),
        out_specs=(P(("grp", "req"), "hd", "seq", None), P(None, ("grp", "req"), "hd", None)),
        check_vma=False,
    )
```

```python
import functools
import math

import jax
import jax.numpy as jnp
from jax import lax
from jax.experimental import pallas as pl
from jax.experimental.pallas import tpu as pltpu
from jax.sharding import PartitionSpec as P

F32 = jnp.float32
BF16 = jnp.bfloat16
NEG = -1e30


def contract_last(a, b):
    return lax.dot_general(a, b, (((1,), (1,)), ((), ())), preferred_element_type=F32)


def softmax_block(query, keys, values, allowed, scale):
    scores = jnp.where(allowed, contract_last(query, keys) * scale, NEG)
    highest = jnp.max(scores, axis=-1, keepdims=True)
    exponent = jnp.exp(scores - highest)
    total = jnp.sum(exponent, axis=-1, keepdims=True)
    weighted = jnp.dot(exponent.astype(BF16), values, preferred_element_type=F32)
    return highest, total, weighted


def kernel(
    shards, cap, groups, owners,
    cache, evicted, weight, target, counts, queries, fresh,
    merged, attended,
    evict_v, weight_v, target_v, counts_v, query_v, fresh_v,
    send, recv, meta_send, meta_recv, query_s, fresh_o, fresh_ml,
    part, part_recv, part_all, result,
    in_sem, cache_sem, row_ssem, row_rsem, meta_ssem, meta_rsem,
    part_ssem, part_rsem, all_ssem, all_rsem, res_ssem, res_rsem,
):
    reqs, heads, kept, width = merged.shape
    pairs = reqs * heads
    evict = evict_v.shape[2]
    steps, _, _, depth = query_v.shape
    rows = query_s.shape[1]
    group = rows // steps
    slots = shards * cap
    per = pairs // owners
    scale = 1.0 / math.sqrt(depth)
    me = lax.axis_index("seq")

    def peer(d):
        return lax.rem(me + d, shards)

    def source(d):
        return lax.rem(me + shards - d, shards)

    def remote(src, dst, ssem, rsem, device):
        return pltpu.make_async_remote_copy(
            src_ref=src, dst_ref=dst, send_sem=ssem, recv_sem=rsem,
            device_id={"seq": device}, device_id_type=pl.DeviceIdType.MESH,
        )

    small = [
        pltpu.make_async_copy(src, dst, in_sem.at[i])
        for i, (src, dst) in enumerate((
            (target, target_v), (weight, weight_v), (evicted, evict_v),
            (queries, query_v), (fresh, fresh_v), (counts, counts_v),
        ))
    ]
    for copy in small:
        copy.start()
    order = []
    shared = min(1, owners - 1)
    for o in [0] * shared + list(range(owners - 1, shared, -1)) + [shared]:
        order += [o * per + j for j in range(per)]
    loads = {}
    for i in order:
        r, h = divmod(i, heads)
        loads[i] = pltpu.make_async_copy(cache.at[r, h], merged.at[r, h], cache_sem.at[i])
        loads[i].start()

    barrier = pltpu.get_barrier_semaphore()
    for d in range(1, shards):
        pl.semaphore_signal(
            barrier, inc=1, device_id={"seq": peer(d)}, device_id_type=pl.DeviceIdType.MESH
        )

    for copy in small[:3]:
        copy.wait()
    aimed = jnp.concatenate([target_v[r] for r in range(reqs)], axis=0)
    weights = jnp.concatenate([weight_v[r].astype(F32) for r in range(reqs)], axis=0)
    owned, position, base = [], jnp.zeros_like(aimed), jnp.zeros(aimed.shape, F32)
    for d in range(shards):
        low = peer(d) * kept
        mine = (aimed >= low) & (aimed < low + kept)
        owned.append(jnp.where(mine, 1.0, 0.0))
        position = jnp.where(mine, aimed - low, position)
        base = jnp.where(mine, float(d * cap), base)
    above = lax.broadcasted_iota(jnp.int32, (evict, evict), 0) < lax.broadcasted_iota(
        jnp.int32, (evict, evict), 1
    )
    earlier = jnp.dot(
        jnp.concatenate(owned, axis=0).astype(BF16),
        jnp.where(above, 1.0, 0.0).astype(BF16),
        preferred_element_type=F32,
    )
    slot = base
    for d in range(shards):
        slot = slot + owned[d] * earlier[d * pairs : (d + 1) * pairs]
    slot = slot.astype(jnp.int32)
    features = jnp.concatenate(
        [weights, (position & 255).astype(F32), (position >> 8).astype(F32)], axis=0
    ).astype(BF16)
    slot_row = lax.broadcasted_iota(jnp.int32, (slots, evict), 0)
    for i in order:
        r, h = divmod(i, heads)
        packing = jnp.where(slot_row == slot[i : i + 1, :], 1.0, 0.0).astype(BF16)
        packed = jnp.dot(packing, evict_v[r, h], preferred_element_type=F32).astype(BF16)
        send[i] = packed
        recv[i, 0:cap, :] = packed[0:cap]
        meta = contract_last(features, packing)
        meta_send[i : i + 1, :] = meta[i : i + 1]
        meta_send[pairs + i : pairs + i + 1, :] = (
            meta[2 * pairs + i : 2 * pairs + i + 1] * 256.0 + meta[pairs + i : pairs + i + 1]
        )

    pl.semaphore_wait(barrier, shards - 1)

    meta_copies = {}
    for d in range(1, shards):
        meta_copies[d] = remote(
            meta_send, meta_recv.at[d], meta_ssem.at[d], meta_rsem.at[d], peer(d)
        )
        meta_copies[d].start()
    span = pairs // groups
    row_copies = {}
    for g in range(groups):
        first = order[g] if groups == pairs else g * span
        for d in range(1, shards):
            lot = (pl.ds(first, span), pl.ds(d * cap, cap))
            row_copies[first, d] = remote(
                send.at[lot], recv.at[lot], row_ssem.at[g, d], row_rsem.at[g, d], peer(d)
            )
            row_copies[first, d].start()

    for copy in small[3:]:
        copy.wait()
    diagonal = lax.broadcasted_iota(jnp.int32, (rows, 128), 0) == lax.broadcasted_iota(
        jnp.int32, (rows, 128), 1
    )

    def to_rows(*columns):
        flat = [jnp.sum(jnp.where(diagonal, c, 0.0), axis=0, keepdims=True) for c in columns]
        return jnp.concatenate(flat + [jnp.zeros((8 - len(flat), 128), F32)], axis=0)

    def to_column(row):
        return jnp.sum(jnp.where(diagonal, row, 0.0), axis=1, keepdims=True)

    padded = -(-steps // 16) * 16
    new_step = lax.broadcasted_iota(jnp.int32, (rows, padded), 1)
    row_index = lax.broadcasted_iota(jnp.int32, (rows, padded), 0)
    allowed = row_index < 0
    for s in range(steps):
        allowed = allowed | ((new_step == s) & (row_index >= s * group))
    for r in range(reqs):
        asked = [query_v[s, r].astype(F32) for s in range(steps)]
        added = [fresh_v[s, r].astype(F32) for s in range(steps)]
        for h in range(heads):
            i = r * heads + h
            query = jnp.concatenate(
                [a[h * group : (h + 1) * group] for a in asked], axis=0
            ).astype(BF16)
            query_s[i] = query
            latest = jnp.concatenate(
                [a[h : h + 1] for a in added] + [jnp.zeros((padded - steps, width), F32)], axis=0
            ).astype(BF16)
            highest, total, weighted = softmax_block(
                query, latest[:, :depth], latest[:, depth:], allowed, scale
            )
            fresh_o[i] = weighted
            fresh_ml[i] = to_rows(highest, total)

    for d in range(1, shards):
        meta_copies[d].wait_recv()
    lane = lax.broadcasted_iota(jnp.int32, (2 * pairs, slots), 1)
    meta = meta_send[...]
    for d in range(1, shards):
        meta = jnp.where(lane >= d * cap, meta_recv[d], meta)
    slot_weight = meta[:pairs]
    slot_position = meta[pairs:].astype(jnp.int32)

    def part_out(i, d):
        j = i % per
        return remote(
            part.at[i], part_all.at[j, d], all_ssem.at[j, d], all_rsem.at[j, d], peer(d)
        )

    kept_row = lax.broadcasted_iota(jnp.int32, (kept, slots), 0)
    kept_lane = lax.broadcasted_iota(jnp.int32, (rows, kept), 1)
    ones = jnp.ones((slots, 128), BF16)
    for n, i in enumerate(order):
        r, h = divmod(i, heads)
        loads[i].wait()
        if groups == pairs:
            for d in range(1, shards):
                row_copies[i, d].wait_recv()
        elif n == 0:
            for copy in row_copies.values():
                copy.wait_recv()
        placing = jnp.where(
            kept_row == slot_position[i : i + 1], slot_weight[i : i + 1], 0.0
        ).astype(BF16)
        summed = jnp.dot(placing, recv[i], preferred_element_type=F32)
        factor = 1.0 / (1.0 + jnp.dot(placing, ones, preferred_element_type=F32))
        factor = jnp.concatenate([factor] * (width // 128), axis=1)
        fused = ((merged[r, h].astype(F32) + summed) * factor).astype(BF16)
        merged[r, h] = fused
        highest, total, weighted = softmax_block(
            query_s[i], fused[:, :depth], fused[:, depth:], kept_lane < counts_v[:, r : r + 1], scale
        )
        part[i, 0:rows, :] = weighted
        part[i, rows : rows + 8, :] = to_rows(highest, total)
        owner, j = divmod(i, per)
        if owner == shared:
            for d in range(1, shards):
                part_out(i, d).start()
            continue
        away = lax.rem(owner - me + shards, shards)

        @pl.when(me != owner)
        def _():
            remote(
                part.at[i], part_recv.at[j, away], part_ssem.at[i], part_rsem.at[j, away], owner
            ).start()

    def part_in(j, d):
        return remote(
            part.at[j], part_recv.at[j, d], part_ssem.at[j], part_rsem.at[j, d], peer(d)
        )

    def res_out(j, d):
        mine = me * per + j
        return remote(
            result.at[mine], result.at[mine], res_ssem.at[j, d], res_rsem.at[j, d], peer(d)
        )

    def res_in(j, d):
        theirs = source(d) * per + j
        return remote(
            result.at[theirs], result.at[theirs], res_ssem.at[j, d], res_rsem.at[j, d], peer(d)
        )

    def only_owners(index, f):
        pl.when((index < owners) & (index != shared))(f)

    def blend_pair(mine, arrived):
        tiles = [fresh_ml[mine], part[mine, rows : rows + 8, :]]
        outs = [fresh_o[mine], part[mine, 0:rows, :]]
        for ref in arrived:
            tiles.append(ref[rows : rows + 8, :])
            outs.append(ref[0:rows, :])
        top = tiles[0][0:1]
        for tile in tiles[1:]:
            top = jnp.maximum(top, tile[0:1])
        shares = [jnp.exp(tile[0:1] - top) for tile in tiles]
        total = shares[0] * tiles[0][1:2]
        for share, tile in zip(shares[1:], tiles[1:]):
            total = total + share * tile[1:2]
        lanes = lax.broadcasted_iota(jnp.int32, total.shape, 1)
        total = jnp.where(lanes < rows, total, 1.0)
        blend = to_column(shares[0] / total) * outs[0]
        for share, out in zip(shares[1:], outs[1:]):
            blend = blend + to_column(share / total) * out
        result[mine] = blend.astype(BF16)

    def combine():
        for j in range(per):
            mine = me * per + j
            for d in range(1, shards):
                part_in(j, d).wait_recv()
            blend_pair(mine, [part_recv.at[j, d] for d in range(1, shards)])
            for d in range(1, shards):
                res_out(j, d).start()

    only_owners(me, combine)
    for j in range(per):
        i = shared * per + j
        for d in range(1, shards):
            part_out(i, d).wait_recv()
        blend_pair(i, [part_all.at[j, d] for d in range(1, shards)])

    for j in range(per):
        for d in range(1, shards):
            only_owners(source(d), lambda: res_in(j, d).wait_recv())
    for r in range(reqs):
        done = [result[r * heads + h].astype(F32) for h in range(heads)]
        for s in range(steps):
            attended[s, r] = jnp.concatenate(
                [a[s * group : (s + 1) * group] for a in done], axis=0
            ).astype(BF16)

    for copy in list(meta_copies.values()) + list(row_copies.values()):
        copy.wait_send()
    for i in order:
        owner = i // per
        if owner == shared:
            for d in range(1, shards):
                part_out(i, d).wait_send()
            continue

        @pl.when(me != owner)
        def _():
            remote(
                part.at[i], part_recv.at[0, 1], part_ssem.at[i], part_rsem.at[0, 1], owner
            ).wait_send()

    def drain():
        for j in range(per):
            for d in range(1, shards):
                res_out(j, d).wait_send()

    only_owners(me, drain)


def write_out(merged, attended, merged_out, attended_out, sem):
    copies = [
        pltpu.make_async_copy(merged, merged_out, sem.at[0]),
        pltpu.make_async_copy(attended, attended_out, sem.at[1]),
    ]
    for copy in copies:
        copy.start()
    for copy in copies:
        copy.wait()


def body(shards, cache, evicted, merge_weight, targets, kept_counts, queries, new_rows):
    reqs, heads, kept, width = cache.shape
    pairs = reqs * heads
    evict = evicted.shape[2]
    steps, _, query_local, depth = queries.shape
    rows = steps * query_local // heads
    cap = -(-max(2, 2 * evict // shards) // 16) * 16
    slots = shards * cap
    groups = pairs if shards <= 8 else 1
    owners = min(shards, pairs)
    per = pairs // owners
    dma = pltpu.SemaphoreType.DMA
    done = pl.pallas_call(
        functools.partial(kernel, shards, cap, groups, owners),
        out_shape=(
            jax.ShapeDtypeStruct(cache.shape, BF16),
            jax.ShapeDtypeStruct(queries.shape, BF16),
        ),
        in_specs=[pl.BlockSpec(memory_space=pltpu.HBM)] * 7,
        out_specs=(pl.BlockSpec(memory_space=pltpu.VMEM),) * 2,
        scratch_shapes=[
            pltpu.VMEM(evicted.shape, BF16),
            pltpu.VMEM(merge_weight.shape, BF16),
            pltpu.VMEM(targets.shape, jnp.int32),
            pltpu.VMEM(kept_counts.shape[::-1], jnp.int32),
            pltpu.VMEM(queries.shape, BF16),
            pltpu.VMEM(new_rows.shape, BF16),
            pltpu.VMEM((pairs, slots, width), BF16),
            pltpu.VMEM((pairs, slots, width), BF16),
            pltpu.VMEM((2 * pairs, slots), F32),
            pltpu.VMEM((shards, 2 * pairs, slots), F32),
            pltpu.VMEM((pairs, rows, depth), BF16),
            pltpu.VMEM((pairs, rows, depth), F32),
            pltpu.VMEM((pairs, 8, 128), F32),
            pltpu.VMEM((pairs, rows + 8, depth), F32),
            pltpu.VMEM((per, shards, rows + 8, depth), F32),
            pltpu.VMEM((per, shards, rows + 8, depth), F32),
            pltpu.VMEM((pairs, rows, depth), BF16),
            dma((6,)),
            dma((pairs,)),
            dma((groups, shards)),
            dma((groups, shards)),
            dma((shards,)),
            dma((shards,)),
            dma((pairs,)),
            dma((per, shards)),
            dma((per, shards)),
            dma((per, shards)),
            dma((per, shards)),
            dma((per, shards)),
        ],
        compiler_params=pltpu.CompilerParams(
            collective_id=0, has_side_effects=True, vmem_limit_bytes=48 * 1024 * 1024
        ),
    )(*(
        pltpu.with_memory_space_constraint(a, pltpu.HBM)
        for a in (cache, evicted, merge_weight, targets, kept_counts.T, queries, new_rows)
    ))
    return pl.pallas_call(
        write_out,
        out_shape=tuple(jax.ShapeDtypeStruct(a.shape, a.dtype) for a in done),
        in_specs=[pl.BlockSpec(memory_space=pltpu.VMEM)] * 2,
        out_specs=(pl.BlockSpec(memory_space=pltpu.HBM),) * 2,
        scratch_shapes=[dma((2,))],
    )(*(pltpu.with_memory_space_constraint(a, pltpu.VMEM) for a in done))


def solution(mesh):
    return jax.shard_map(
        functools.partial(body, mesh.shape["seq"]),
        mesh=mesh,
        in_specs=(
            P(("grp", "req"), "hd", "seq", None),
            P(("grp", "req"), "hd", "seq", None),
            P(("grp", "req"), "hd", "seq"),
            P(("grp", "req"), "hd", "seq"),
            P(("grp", "req"), "seq"),
            P(None, ("grp", "req"), "hd", None),
            P(None, ("grp", "req"), "hd", None),
        ),
        out_specs=(P(("grp", "req"), "hd", "seq", None), P(None, ("grp", "req"), "hd", None)),
        check_vma=False,
    )
```

```python
import functools
import math

import jax
import jax.numpy as jnp
from jax import lax
from jax.experimental import pallas as pl
from jax.experimental.pallas import tpu as pltpu
from jax.sharding import PartitionSpec as P

F32 = jnp.float32
BF16 = jnp.bfloat16
NEG = -1e30


def contract_last(a, b):
    return lax.dot_general(a, b, (((1,), (1,)), ((), ())), preferred_element_type=F32)


def softmax_block(query, keys, values, allowed, scale):
    scores = jnp.where(allowed, contract_last(query, keys) * scale, NEG)
    highest = jnp.max(scores, axis=-1, keepdims=True)
    exponent = jnp.exp(scores - highest)
    total = jnp.sum(exponent, axis=-1, keepdims=True)
    weighted = jnp.dot(exponent.astype(BF16), values, preferred_element_type=F32)
    return highest, total, weighted


def kernel(
    shards, cap, groups, owners,
    cache, evicted, weight, target, counts, queries, fresh,
    merged, attended,
    evict_v, weight_v, target_v, counts_v, query_v, fresh_v,
    send, recv, meta_send, meta_recv, query_s, fresh_o, fresh_ml,
    relay, part, part_recv, result,
    in_sem, cache_sem, row_ssem, row_rsem, hop_ssem, hop_rsem, fwd_ssem,
    meta_ssem, meta_rsem,
    part_ssem, part_rsem, res_ssem, res_rsem,
):
    reqs, heads, kept, width = merged.shape
    pairs = reqs * heads
    evict = evict_v.shape[2]
    steps, _, _, depth = query_v.shape
    rows = query_s.shape[1]
    group = rows // steps
    slots = shards * cap
    per = pairs // owners
    scale = 1.0 / math.sqrt(depth)
    me = lax.axis_index("seq")

    def peer(d):
        return lax.rem(me + d, shards)

    def source(d):
        return lax.rem(me + shards - d, shards)

    def remote(src, dst, ssem, rsem, device):
        return pltpu.make_async_remote_copy(
            src_ref=src, dst_ref=dst, send_sem=ssem, recv_sem=rsem,
            device_id={"seq": device}, device_id_type=pl.DeviceIdType.MESH,
        )

    small = [
        pltpu.make_async_copy(src, dst, in_sem.at[i])
        for i, (src, dst) in enumerate((
            (target, target_v), (weight, weight_v), (evicted, evict_v),
            (queries, query_v), (fresh, fresh_v), (counts, counts_v),
        ))
    ]
    for copy in small:
        copy.start()
    order = []
    for o in [0] + list(range(owners - 1, 0, -1)):
        order += [o * per + j for j in range(per)]
    loads = {}
    for i in order:
        r, h = divmod(i, heads)
        loads[i] = pltpu.make_async_copy(cache.at[r, h], merged.at[r, h], cache_sem.at[i])
        loads[i].start()

    barrier = pltpu.get_barrier_semaphore()
    for d in range(1, shards):
        pl.semaphore_signal(
            barrier, inc=1, device_id={"seq": peer(d)}, device_id_type=pl.DeviceIdType.MESH
        )

    for copy in small[:3]:
        copy.wait()
    aimed = jnp.concatenate([target_v[r] for r in range(reqs)], axis=0)
    weights = jnp.concatenate([weight_v[r].astype(F32) for r in range(reqs)], axis=0)
    owned, position, base = [], jnp.zeros_like(aimed), jnp.zeros(aimed.shape, F32)
    for d in range(shards):
        low = peer(d) * kept
        mine = (aimed >= low) & (aimed < low + kept)
        owned.append(jnp.where(mine, 1.0, 0.0))
        position = jnp.where(mine, aimed - low, position)
        base = jnp.where(mine, float(d * cap), base)
    above = lax.broadcasted_iota(jnp.int32, (evict, evict), 0) < lax.broadcasted_iota(
        jnp.int32, (evict, evict), 1
    )
    earlier = jnp.dot(
        jnp.concatenate(owned, axis=0).astype(BF16),
        jnp.where(above, 1.0, 0.0).astype(BF16),
        preferred_element_type=F32,
    )
    slot = base
    for d in range(shards):
        slot = slot + owned[d] * earlier[d * pairs : (d + 1) * pairs]
    slot = slot.astype(jnp.int32)
    features = jnp.concatenate(
        [weights, (position & 255).astype(F32), (position >> 8).astype(F32)], axis=0
    ).astype(BF16)
    slot_row = lax.broadcasted_iota(jnp.int32, (slots, evict), 0)
    for i in order:
        r, h = divmod(i, heads)
        packing = jnp.where(slot_row == slot[i : i + 1, :], 1.0, 0.0).astype(BF16)
        packed = jnp.dot(packing, evict_v[r, h], preferred_element_type=F32).astype(BF16)
        send[i] = packed
        recv[i, 0:cap, :] = packed[0:cap]
        meta = contract_last(features, packing)
        meta_send[i : i + 1, :] = meta[i : i + 1]
        meta_send[pairs + i : pairs + i + 1, :] = (
            meta[2 * pairs + i : 2 * pairs + i + 1] * 256.0 + meta[pairs + i : pairs + i + 1]
        )

    pl.semaphore_wait(barrier, shards - 1)

    meta_copies = {}
    for d in range(1, shards):
        meta_copies[d] = remote(
            meta_send, meta_recv.at[d], meta_ssem.at[d], meta_rsem.at[d], peer(d)
        )
        meta_copies[d].start()
    span = pairs // groups
    middle = shards // 2
    bounce = groups == pairs and shards >= 4 and shards % 2 == 0
    late = order[pairs - pairs // 2 :] if bounce else []

    def hop_in(k, i):
        return remote(
            send.at[i, pl.ds(middle * cap, cap)], relay.at[k],
            hop_ssem.at[k], hop_rsem.at[k], peer(shards - 1),
        )

    def hop_out(k, i):
        return remote(
            relay.at[k], recv.at[i, pl.ds(middle * cap, cap)],
            fwd_ssem.at[k], row_rsem.at[order.index(i), middle], peer(middle + 1),
        )

    for k, i in enumerate(late):
        hop_in(k, i).start()
    row_copies, sent = {}, []

    def send_rows(part_of, distances):
        for g in part_of:
            first = order[g] if groups == pairs else g * span
            for d in distances:
                lot = (pl.ds(first, span), pl.ds(d * cap, cap))
                copy = remote(
                    send.at[lot], recv.at[lot], row_ssem.at[g, d], row_rsem.at[g, d], peer(d)
                )
                row_copies[first, d] = copy
                if first in late and d == middle:
                    continue
                copy.start()
                sent.append(copy)

    early = groups - len(late)
    send_rows(range(early), range(1, shards))
    send_rows(range(early, groups), range(1, middle + 1))

    for copy in small[3:]:
        copy.wait()
    diagonal = lax.broadcasted_iota(jnp.int32, (rows, 128), 0) == lax.broadcasted_iota(
        jnp.int32, (rows, 128), 1
    )

    def to_rows(*columns):
        flat = [jnp.sum(jnp.where(diagonal, c, 0.0), axis=0, keepdims=True) for c in columns]
        return jnp.concatenate(flat + [jnp.zeros((8 - len(flat), 128), F32)], axis=0)

    def to_column(row):
        return jnp.sum(jnp.where(diagonal, row, 0.0), axis=1, keepdims=True)

    padded = -(-steps // 16) * 16
    new_step = lax.broadcasted_iota(jnp.int32, (rows, padded), 1)
    row_index = lax.broadcasted_iota(jnp.int32, (rows, padded), 0)
    allowed = row_index < 0
    for s in range(steps):
        allowed = allowed | ((new_step == s) & (row_index >= s * group))
    for r in range(reqs):
        asked = [query_v[s, r].astype(F32) for s in range(steps)]
        added = [fresh_v[s, r].astype(F32) for s in range(steps)]
        for h in range(heads):
            i = r * heads + h
            query = jnp.concatenate(
                [a[h * group : (h + 1) * group] for a in asked], axis=0
            ).astype(BF16)
            query_s[i] = query
            latest = jnp.concatenate(
                [a[h : h + 1] for a in added] + [jnp.zeros((padded - steps, width), F32)], axis=0
            ).astype(BF16)
            highest, total, weighted = softmax_block(
                query, latest[:, :depth], latest[:, depth:], allowed, scale
            )
            fresh_o[i] = weighted
            fresh_ml[i] = to_rows(highest, total)

    for k, i in enumerate(late):
        hop_in(k, i).wait_recv()
        hop_out(k, i).start()
    send_rows(range(early, groups), range(middle + 1, shards))
    for d in range(1, shards):
        meta_copies[d].wait_recv()
    lane = lax.broadcasted_iota(jnp.int32, (2 * pairs, slots), 1)
    meta = meta_send[...]
    for d in range(1, shards):
        meta = jnp.where(lane >= d * cap, meta_recv[d], meta)
    slot_weight = meta[:pairs]
    slot_position = meta[pairs:].astype(jnp.int32)

    kept_row = lax.broadcasted_iota(jnp.int32, (kept, slots), 0)
    kept_lane = lax.broadcasted_iota(jnp.int32, (rows, kept), 1)
    ones = jnp.ones((slots, 128), BF16)
    for n, i in enumerate(order):
        r, h = divmod(i, heads)
        loads[i].wait()
        if groups == pairs:
            for d in range(1, shards):
                row_copies[i, d].wait_recv()
        elif n == 0:
            for copy in row_copies.values():
                copy.wait_recv()
        placing = jnp.where(
            kept_row == slot_position[i : i + 1], slot_weight[i : i + 1], 0.0
        ).astype(BF16)
        summed = jnp.dot(placing, recv[i], preferred_element_type=F32)
        factor = 1.0 / (1.0 + jnp.dot(placing, ones, preferred_element_type=F32))
        factor = jnp.concatenate([factor] * (width // 128), axis=1)
        fused = ((merged[r, h].astype(F32) + summed) * factor).astype(BF16)
        merged[r, h] = fused
        highest, total, weighted = softmax_block(
            query_s[i], fused[:, :depth], fused[:, depth:], kept_lane < counts_v[:, r : r + 1], scale
        )
        part[i, 0:rows, :] = weighted
        part[i, rows : rows + 8, :] = to_rows(highest, total)
        owner, j = divmod(i, per)
        away = lax.rem(owner - me + shards, shards)

        @pl.when(me != owner)
        def _():
            remote(
                part.at[i], part_recv.at[j, away], part_ssem.at[i], part_rsem.at[j, away], owner
            ).start()

    def part_in(j, d):
        return remote(
            part.at[j], part_recv.at[j, d], part_ssem.at[j], part_rsem.at[j, d], peer(d)
        )

    def res_out(j, d):
        mine = me * per + j
        return remote(
            result.at[mine], result.at[mine], res_ssem.at[j, d], res_rsem.at[j, d], peer(d)
        )

    def res_in(j, d):
        theirs = source(d) * per + j
        return remote(
            result.at[theirs], result.at[theirs], res_ssem.at[j, d], res_rsem.at[j, d], peer(d)
        )

    def only_owners(index, f):
        if owners == shards:
            f()
        else:
            pl.when(index < owners)(f)

    def combine():
        for j in range(per):
            mine = me * per + j
            for d in range(1, shards):
                part_in(j, d).wait_recv()
            tiles = [fresh_ml[mine], part[mine, rows : rows + 8, :]]
            outs = [fresh_o[mine], part[mine, 0:rows, :]]
            for d in range(1, shards):
                tiles.append(part_recv[j, d, rows : rows + 8, :])
                outs.append(part_recv[j, d, 0:rows, :])
            top = tiles[0][0:1]
            for tile in tiles[1:]:
                top = jnp.maximum(top, tile[0:1])
            shares = [jnp.exp(tile[0:1] - top) for tile in tiles]
            total = shares[0] * tiles[0][1:2]
            for share, tile in zip(shares[1:], tiles[1:]):
                total = total + share * tile[1:2]
            lanes = lax.broadcasted_iota(jnp.int32, total.shape, 1)
            total = jnp.where(lanes < rows, total, 1.0)
            blend = to_column(shares[0] / total) * outs[0]
            for share, out in zip(shares[1:], outs[1:]):
                blend = blend + to_column(share / total) * out
            result[mine] = blend.astype(BF16)
            for d in range(1, shards):
                res_out(j, d).start()

    only_owners(me, combine)

    for j in range(per):
        for d in range(1, shards):
            only_owners(source(d), lambda: res_in(j, d).wait_recv())
    for r in range(reqs):
        done = [result[r * heads + h].astype(F32) for h in range(heads)]
        for s in range(steps):
            attended[s, r] = jnp.concatenate(
                [a[s * group : (s + 1) * group] for a in done], axis=0
            ).astype(BF16)

    for copy in list(meta_copies.values()) + sent:
        copy.wait_send()
    for k, i in enumerate(late):
        hop_in(k, i).wait_send()
        hop_out(k, i).wait_send()
    for i in order:
        owner = i // per

        @pl.when(me != owner)
        def _():
            remote(
                part.at[i], part_recv.at[0, 1], part_ssem.at[i], part_rsem.at[0, 1], owner
            ).wait_send()

    def drain():
        for j in range(per):
            for d in range(1, shards):
                res_out(j, d).wait_send()

    only_owners(me, drain)


def write_out(merged, attended, merged_out, attended_out, sem):
    copies = [
        pltpu.make_async_copy(merged, merged_out, sem.at[0]),
        pltpu.make_async_copy(attended, attended_out, sem.at[1]),
    ]
    for copy in copies:
        copy.start()
    for copy in copies:
        copy.wait()


def body(shards, cache, evicted, merge_weight, targets, kept_counts, queries, new_rows):
    reqs, heads, kept, width = cache.shape
    pairs = reqs * heads
    evict = evicted.shape[2]
    steps, _, query_local, depth = queries.shape
    rows = steps * query_local // heads
    cap = -(-max(2, 2 * evict // shards) // 16) * 16
    slots = shards * cap
    groups = pairs if shards <= 8 else 1
    owners = min(shards, pairs)
    per = pairs // owners
    dma = pltpu.SemaphoreType.DMA
    done = pl.pallas_call(
        functools.partial(kernel, shards, cap, groups, owners),
        out_shape=(
            jax.ShapeDtypeStruct(cache.shape, BF16),
            jax.ShapeDtypeStruct(queries.shape, BF16),
        ),
        in_specs=[pl.BlockSpec(memory_space=pltpu.HBM)] * 7,
        out_specs=(pl.BlockSpec(memory_space=pltpu.VMEM),) * 2,
        scratch_shapes=[
            pltpu.VMEM(evicted.shape, BF16),
            pltpu.VMEM(merge_weight.shape, BF16),
            pltpu.VMEM(targets.shape, jnp.int32),
            pltpu.VMEM(kept_counts.shape[::-1], jnp.int32),
            pltpu.VMEM(queries.shape, BF16),
            pltpu.VMEM(new_rows.shape, BF16),
            pltpu.VMEM((pairs, slots, width), BF16),
            pltpu.VMEM((pairs, slots, width), BF16),
            pltpu.VMEM((2 * pairs, slots), F32),
            pltpu.VMEM((shards, 2 * pairs, slots), F32),
            pltpu.VMEM((pairs, rows, depth), BF16),
            pltpu.VMEM((pairs, rows, depth), F32),
            pltpu.VMEM((pairs, 8, 128), F32),
            pltpu.VMEM((max(1, pairs // 2), cap, width), BF16),
            pltpu.VMEM((pairs, rows + 8, depth), F32),
            pltpu.VMEM((per, shards, rows + 8, depth), F32),
            pltpu.VMEM((pairs, rows, depth), BF16),
            dma((6,)),
            dma((pairs,)),
            dma((groups, shards)),
            dma((groups, shards)),
            dma((max(1, pairs // 2),)),
            dma((max(1, pairs // 2),)),
            dma((max(1, pairs // 2),)),
            dma((shards,)),
            dma((shards,)),
            dma((pairs,)),
            dma((per, shards)),
            dma((per, shards)),
            dma((per, shards)),
        ],
        compiler_params=pltpu.CompilerParams(
            collective_id=0, has_side_effects=True, vmem_limit_bytes=48 * 1024 * 1024
        ),
    )(*(
        pltpu.with_memory_space_constraint(a, pltpu.HBM)
        for a in (cache, evicted, merge_weight, targets, kept_counts.T, queries, new_rows)
    ))
    return pl.pallas_call(
        write_out,
        out_shape=tuple(jax.ShapeDtypeStruct(a.shape, a.dtype) for a in done),
        in_specs=[pl.BlockSpec(memory_space=pltpu.VMEM)] * 2,
        out_specs=(pl.BlockSpec(memory_space=pltpu.HBM),) * 2,
        scratch_shapes=[dma((2,))],
    )(*(pltpu.with_memory_space_constraint(a, pltpu.VMEM) for a in done))


def solution(mesh):
    return jax.shard_map(
        functools.partial(body, mesh.shape["seq"]),
        mesh=mesh,
        in_specs=(
            P(("grp", "req"), "hd", "seq", None),
            P(("grp", "req"), "hd", "seq", None),
            P(("grp", "req"), "hd", "seq"),
            P(("grp", "req"), "hd", "seq"),
            P(("grp", "req"), "seq"),
            P(None, ("grp", "req"), "hd", None),
            P(None, ("grp", "req"), "hd", None),
        ),
        out_specs=(P(("grp", "req"), "hd", "seq", None), P(None, ("grp", "req"), "hd", None)),
        check_vma=False,
    )
```
